32 devices in a mesh: groups: 2 (over x), row: 16 (over z, y, core).
Axes of the slice: x: 2, y: 2, z: 4, core: 2. Of those that a mesh axis runs over, the one named last changes fastest.
Arguments:
- matrix: float32 [32768, 1024], P(('groups', 'row')), parts along dimension 0, may hold values from -6 to 6
- leaf_vectors: float32 [4, 10240, 256], P('groups', 'row'), parts along dimension 0, may hold values from -0.25 to 0.25
- leaf_factors: float32 [4, 4096, 256], P('groups', 'row'), parts along dimension 0, as said below
- tree_vectors: float32 [4, 4096, 256], P('groups', 'row'), parts along dimension 0, may hold values from -0.375 to 0.375
- tree_factors: float32 [4, 4096, 256], P('groups', 'row'), parts along dimension 0, as said below
- leaf_blocks: int32 [4, 80], P('groups', 'row'), parts along dimension 0, may hold values from 0 to 7, as said below
- owner: int32 [4], P('groups'), parts along dimension 0, may hold values from 0 to 15
Outputs:
- updated: float32 [32768, 1024], P(('groups', 'row')), parts along dimension 0
The draws below stay inside these ranges and needn't reach their ends.
There are 2 independent parts, one for each index of `groups`. The reference program is written for one: setup_inputs(seed, part) draws one part's arguments, and reference() takes and returns one part's arrays. A program takes and returns all parts, laid end to end along the dimension named above; each array names one. Nothing has to cross between parts.
Inputs may be any that keep to these rules, and one draw needn't show every extreme that they name: `leaf_blocks`: in step s, the 5 entries of each grid block are distinct row-block numbers of that block: first the 2 blocks of the step's panel rows in order, last the block's final row block, the others between them. `leaf_factors`: each 256 x 256 factor is upper triangular. `tree_factors`: each 256 x 256 factor is upper triangular.
All inputs are finite; a program needn't handle non-finite values.
Results may differ from the reference program's by a relative error of at most 0.0001.
Values sent between devices are 32-bit elements; how exact they have to be, the bound alone decides.
A program may use at most 128 MiB of HBM per device.

```python
import math
import jax
import jax.numpy as jnp
from jax import lax

PW = 256
COLS = 1024
BLK = 128
NB = 5
STEPS = 2
ROWS_DEV = 1024
LEVELS = 4
ROWS = 16384
LEAF_ROWS = 10240
FACT_ROWS = 4096
BLOCK_LIST = 80
N_ROW = 16


def triangle(key):
    factor_count = FACT_ROWS // PW
    diag_key, off_key = jax.random.split(key)
    diagonal_part = jax.random.uniform(diag_key, (STEPS, factor_count, PW), jnp.float32, 0.5, 1.0)
    off_part = jax.random.normal(off_key, (STEPS, factor_count, PW, PW), jnp.float32) * (0.4 / math.sqrt(PW))
    row_index = lax.broadcasted_iota(jnp.int32, (PW, PW), 0)
    col_index = lax.broadcasted_iota(jnp.int32, (PW, PW), 1)
    triangular = jnp.where(col_index > row_index, off_part, 0.0)
    triangular = triangular + jnp.where(col_index == row_index, diagonal_part[..., :, None], 0.0)
    return triangular.reshape(STEPS, FACT_ROWS, PW).astype(jnp.float32)


def draw_leaf_factors(key, part):
    return triangle(jax.random.fold_in(key, 11))


def draw_tree_factors(key, part):
    return triangle(jax.random.fold_in(key, 23))


def draw_leaf_blocks(key, part):
    devices = BLOCK_LIST // NB
    block_count = ROWS_DEV // BLK
    per_panel = PW // BLK
    free_count = NB - per_panel - 1
    rows_out = []
    for step_index in range(STEPS):
        scores = jax.random.randint(jax.random.fold_in(key, 31 + step_index), (devices, block_count), 0, 1048576)
        col_index = lax.broadcasted_iota(jnp.int32, (devices, block_count), 1)
        scores = scores * block_count + col_index
        allowed = (col_index >= (step_index + 1) * per_panel) & (col_index <= block_count - 2)
        scores = jnp.where(allowed, scores, -1 - col_index)
        chosen = lax.top_k(scores, free_count)[1].astype(jnp.int32)
        panel_part = step_index * per_panel + lax.broadcasted_iota(jnp.int32, (devices, per_panel), 1)
        last_part = jnp.full((devices, 1), block_count - 1, jnp.int32)
        listed = jnp.concatenate([panel_part, chosen, last_part], axis=1)
        rows_out.append(listed.reshape(-1))
    return jnp.stack(rows_out).astype(jnp.int32)


def shard_levels(rng, extent, pieces, low, high):
    loudness = 1.0
    for dim, shards_of in pieces:
        heights = jax.random.uniform(jax.random.fold_in(jax.random.fold_in(rng, 6), dim), (shards_of,), jnp.float32, low / len(pieces), high / len(pieces))
        loudness = loudness * jnp.repeat(jnp.exp(heights), extent[dim] // shards_of).reshape((-1,) + (1,) * (len(extent) - 1 - dim))
    return loudness


def noise(own_key, dims, width, limit, cuts=(), kind=jnp.bfloat16):
    values = jax.random.normal(own_key, dims, jnp.float32) * width
    if len(cuts) > 0:
        values = shard_levels(own_key, dims, cuts, -0.22, 0.18) * values
    return jnp.clip(values, min=-limit, max=limit).astype(kind)


def setup_inputs(seed: int = 0, part: int = 0) -> dict:
    seeds = jax.random.split(jax.random.key(seed), 8)
    part_keys = jax.random.split(jax.random.fold_in(seeds[7], part), 8)
    matrix = noise(part_keys[0], (ROWS, COLS), 1.0, 6.0, ((0, 16),), jnp.float32)
    leaf_vectors = noise(part_keys[1], (STEPS, LEAF_ROWS, PW), (NB * BLK) ** -0.5, 0.25, ((1, 16),), jnp.float32)
    leaf_factors = draw_leaf_factors(jax.random.fold_in(jax.random.fold_in(seeds[7], part), 71), part)
    tree_vectors = noise(part_keys[3], (STEPS, FACT_ROWS, PW), PW ** -0.5, 0.375, ((1, 16),), jnp.float32)
    tree_factors = draw_tree_factors(jax.random.fold_in(jax.random.fold_in(seeds[7], part), 71), part)
    leaf_blocks = draw_leaf_blocks(jax.random.fold_in(jax.random.fold_in(seeds[7], part), 71), part)
    owner = jax.random.randint(part_keys[6], (STEPS,), 0, N_ROW).astype(jnp.int32)
    return {"matrix": matrix, "leaf_vectors": leaf_vectors, "leaf_factors": leaf_factors, "tree_vectors": tree_vectors, "tree_factors": tree_factors, "leaf_blocks": leaf_blocks, "owner": owner}


def product(spec_text, left_side, right_side):
    return jnp.einsum(spec_text, left_side, right_side, precision=lax.Precision.HIGHEST)


def tree_combine(top_rows, tree_y, tree_t, owner_now):
    relative_tops = jnp.roll(top_rows, -owner_now, axis=0)
    relative_y = jnp.roll(tree_y, -owner_now, axis=0)
    relative_t = jnp.roll(tree_t, -owner_now, axis=0)
    for tree_level in range(LEVELS):
        partner_gap = 2 ** tree_level
        pair_count = N_ROW // (2 * partner_gap)
        grouped = relative_tops.reshape(pair_count, 2, partner_gap, PW, COLS)
        upper_rows = grouped[:, 0, 0]
        lower_rows = grouped[:, 1, 0]
        vector_lower = relative_y.reshape(pair_count, 2, partner_gap, PW, PW)[:, 1, 0]
        factor_lower = relative_t.reshape(pair_count, 2, partner_gap, PW, PW)[:, 1, 0]
        projected = product("gkp,gkc->gpc", vector_lower, lower_rows)
        update = product("gkp,gkc->gpc", factor_lower, upper_rows + projected)
        grouped = grouped.at[:, 0, 0].set(upper_rows - update)
        grouped = grouped.at[:, 1, 0].set(lower_rows - product("gpk,gkc->gpc", vector_lower, update))
        relative_tops = grouped.reshape(N_ROW, PW, COLS)
    return jnp.roll(relative_tops, owner_now, axis=0)


def reference(matrix, leaf_vectors, leaf_factors, tree_vectors, tree_factors, leaf_blocks, owner):
    block_count = ROWS_DEV // BLK
    work_matrix = matrix.reshape(N_ROW, block_count, BLK, COLS)
    device_ids = jnp.arange(N_ROW).astype(jnp.int32)[:, None]
    for step_index in range(STEPS):
        listed = leaf_blocks[step_index].reshape(N_ROW, NB).astype(jnp.int32)
        gathered = work_matrix[device_ids, listed].reshape(N_ROW, NB * BLK, COLS)
        vectors = leaf_vectors[step_index].reshape(N_ROW, NB * BLK, PW)
        factors = leaf_factors[step_index].reshape(N_ROW, PW, PW)
        projected = product("nrp,nrc->npc", vectors, gathered)
        update = product("nkp,nkc->npc", factors, projected)
        renewed = gathered - product("nrp,npc->nrc", vectors, update)
        work_matrix = work_matrix.at[device_ids, listed].set(renewed.reshape(N_ROW, NB, BLK, COLS))
        by_device = work_matrix.reshape(N_ROW, ROWS_DEV, COLS)
        top_rows = by_device[:, step_index * PW:(step_index + 1) * PW]
        top_rows = tree_combine(top_rows, tree_vectors[step_index].reshape(N_ROW, PW, PW),
                                tree_factors[step_index].reshape(N_ROW, PW, PW), owner[step_index])
        by_device = by_device.at[:, step_index * PW:(step_index + 1) * PW].set(top_rows)
        work_matrix = by_device.reshape(N_ROW, block_count, BLK, COLS)
    return work_matrix.reshape(N_ROW * ROWS_DEV, COLS)
```

```python
import functools

import jax
import jax.numpy as jnp
from jax import lax
from jax.experimental import pallas as pl
from jax.experimental.pallas import tpu as pltpu
from jax.sharding import PartitionSpec as P

BLK = 128
STEPS = 2
COLS_PER_LEAF = 256

NN = (((1,), (0,)), ((), ()))
TN = (((0,), (0,)), ((), ()))
NT = (((1,), (1,)), ((), ()))


def split(value):
    high = value.astype(jnp.bfloat16)
    low = (value - high.astype(jnp.float32)).astype(jnp.bfloat16)
    return high, low


def product3(left, right, dims):
    def one(a, b):
        return lax.dot_general(a, b, dims, preferred_element_type=jnp.float32)

    return one(left[0], right[0]) + (one(left[0], right[1]) + one(left[1], right[0]))


def leaf_kernel(listed, m_ref, y_ref, l_ref, out_ref, tops_ref, yh, yl, yth, ytl, lth, ltl):
    panel = l_ref.shape[1]
    listed_count = y_ref.shape[1] // BLK

    @pl.when(pl.program_id(0) == 0)
    def _():
        for s in range(STEPS):
            high, low = split(y_ref[s])
            yh[s], yl[s] = high, low
            high, low = split(y_ref[s].T)
            yth[s], ytl[s] = high, low
            high, low = split(l_ref[s].T)
            lth[s], ltl[s] = high, low

    out_ref[...] = m_ref[...]
    for s in range(STEPS):
        starts = [pl.multiple_of(listed[s, k] * BLK, BLK) for k in range(listed_count)]
        gathered = jnp.concatenate([out_ref[pl.ds(start, BLK), :] for start in starts], axis=0)
        projected = product3((yth[s], ytl[s]), split(gathered), NN)
        update = product3((lth[s], ltl[s]), split(projected), NN)
        renewed = gathered - product3((yh[s], yl[s]), split(update), NN)
        for k, start in enumerate(starts):
            out_ref[pl.ds(start, BLK), :] = renewed[k * BLK : (k + 1) * BLK]
    for s in range(STEPS):
        tops_ref[:, s * panel : (s + 1) * panel] = out_ref[s * panel : (s + 1) * panel, :].T


def leaf(matrix, leaf_vectors, leaf_factors, leaf_blocks):
    rows, columns = matrix.shape
    width = COLS_PER_LEAF
    steps, leaf_rows, panel = leaf_vectors.shape
    return pl.pallas_call(
        leaf_kernel,
        out_shape=(
            jax.ShapeDtypeStruct((rows, columns), jnp.float32),
            jax.ShapeDtypeStruct((columns, steps * panel), jnp.float32),
        ),
        grid_spec=pltpu.PrefetchScalarGridSpec(
            num_scalar_prefetch=1,
            grid=(columns // width,),
            in_specs=[
                pl.BlockSpec((rows, width), lambda c, *_: (0, c)),
                pl.BlockSpec(leaf_vectors.shape, lambda c, *_: (0, 0, 0)),
                pl.BlockSpec(leaf_factors.shape, lambda c, *_: (0, 0, 0)),
            ],
            out_specs=[
                pl.BlockSpec((rows, width), lambda c, *_: (0, c)),
                pl.BlockSpec((width, steps * panel), lambda c, *_: (c, 0)),
            ],
            scratch_shapes=[
                pltpu.VMEM((steps, leaf_rows, panel), jnp.bfloat16),
                pltpu.VMEM((steps, leaf_rows, panel), jnp.bfloat16),
                pltpu.VMEM((steps, panel, leaf_rows), jnp.bfloat16),
                pltpu.VMEM((steps, panel, leaf_rows), jnp.bfloat16),
                pltpu.VMEM((steps, panel, panel), jnp.bfloat16),
                pltpu.VMEM((steps, panel, panel), jnp.bfloat16),
            ],
        ),
    )(leaf_blocks, matrix, leaf_vectors, leaf_factors)


def tree_kernel(upper, lower, x_ref, u_ref, f_ref, out_ref):
    node, step = pl.program_id(0), pl.program_id(1)
    panel = u_ref.shape[2]
    half = panel // 2

    @pl.when((node == 0) & (step == 0))
    def _():
        out_ref[...] = x_ref[...]

    u = split(u_ref[0, 0])
    packed = f_ref[0, 0]
    bottom = jnp.concatenate([jnp.zeros((half, half), jnp.float32), packed[:, panel:]], axis=1)
    f = split(jnp.concatenate([packed[:, :panel], bottom], axis=0))
    for s in range(STEPS):

        @pl.when(step == s)
        def _():
            place = pl.ds(s * panel, panel)
            a, b = upper[s, node], lower[s, node]
            xa, xb = out_ref[a, :, place], out_ref[b, :, place]
            total = xa + product3(split(xb), u, NN)
            w = product3(split(total), f, NN)
            out_ref[a, :, place] = xa - w
            out_ref[b, :, place] = xb - product3(split(w), u, NT)


def tree(gathered, vectors, factors, upper, lower):
    devices, steps, panel, _ = vectors.shape
    return pl.pallas_call(
        tree_kernel,
        out_shape=jax.ShapeDtypeStruct(gathered.shape, jnp.float32),
        grid_spec=pltpu.PrefetchScalarGridSpec(
            num_scalar_prefetch=2,
            grid=(devices - 1, steps),
            in_specs=[
                pl.BlockSpec(gathered.shape, lambda n, s, *_: (0, 0, 0)),
                pl.BlockSpec((1, 1, panel, panel), lambda n, s, up, lo: (lo[s, n], s, 0, 0)),
                pl.BlockSpec((1, 1) + factors.shape[2:], lambda n, s, up, lo: (lo[s, n], s, 0, 0)),
            ],
            out_specs=pl.BlockSpec(gathered.shape, lambda n, s, *_: (0, 0, 0)),
        ),
    )(upper, lower, gathered, vectors, factors)


def place_kernel(t_ref, _, out_ref):
    out_ref[...] = t_ref[...].T


def place(tops, work):
    columns, rows = tops.shape
    width = 256
    return pl.pallas_call(
        place_kernel,
        out_shape=jax.ShapeDtypeStruct(work.shape, jnp.float32),
        grid=(columns // width,),
        in_specs=[
            pl.BlockSpec((width, rows), lambda c: (c, 0)),
            pl.BlockSpec(memory_space=pl.ANY),
        ],
        out_specs=pl.BlockSpec((rows, width), lambda c: (0, c)),
        input_output_aliases={1: 0},
    )(tops, work)


def pairs(row_count):
    uppers, lowers = [], []
    gap = 1
    while gap < row_count:
        for start in range(0, row_count, 2 * gap):
            uppers.append(start)
            lowers.append(start + gap)
        gap *= 2
    return jnp.array(uppers, jnp.int32), jnp.array(lowers, jnp.int32)


def shards(matrix, leaf_vectors, leaf_factors, tree_vectors, tree_factors, leaf_blocks, owner):
    row_count = lax.axis_size("row")
    columns = matrix.shape[1]
    panel = tree_vectors.shape[2]
    half = panel // 2
    packed = jnp.concatenate([tree_factors[:, :half], tree_factors[:, half:, half:]], axis=2)
    vectors = lax.all_gather(tree_vectors, "row")
    factors = lax.all_gather(packed, "row")
    work, tops = leaf(matrix, leaf_vectors, leaf_factors, leaf_blocks)
    spread = tops.reshape(row_count, columns // row_count, STEPS * panel)
    gathered = lax.all_to_all(spread, "row", 0, 0)
    uppers, lowers = pairs(row_count)
    upper = (uppers[None] + owner[:, None]) % row_count
    lower = (lowers[None] + owner[:, None]) % row_count
    done = tree(gathered, vectors, factors, upper, lower)
    back = lax.all_to_all(done, "row", 0, 0)
    return place(back.reshape(columns, STEPS * panel), work)


def solution(mesh):
    return jax.shard_map(
        shards,
        mesh=mesh,
        in_specs=(
            P(("groups", "row"), None),
            P("groups", "row", None),
            P("groups", "row", None),
            P("groups", "row", None),
            P("groups", "row", None),
            P("groups", "row"),
            P("groups"),
        ),
        out_specs=P(("groups", "row"), None),
        check_vma=False,
    )
```

```python
import functools

import jax
import jax.numpy as jnp
from jax import lax
from jax.experimental import pallas as pl
from jax.experimental.pallas import tpu as pltpu
from jax.sharding import PartitionSpec as P

BLK = 128
STEPS = 2
COLS_PER_LEAF = 256

NN = (((1,), (0,)), ((), ()))
TN = (((0,), (0,)), ((), ()))
NT = (((1,), (1,)), ((), ()))


def split(value):
    high = value.astype(jnp.bfloat16)
    low = (value - high.astype(jnp.float32)).astype(jnp.bfloat16)
    return high, low


def product3(left, right, dims):
    def one(a, b):
        return lax.dot_general(a, b, dims, preferred_element_type=jnp.float32)

    return one(left[0], right[0]) + (one(left[0], right[1]) + one(left[1], right[0]))


def leaf_kernel(listed, odd, m_ref, y_ref, l_ref, u_ref, out_ref, *rest):
    tops_refs, (yh, yl, yth, ytl, lth, ltl) = rest[:STEPS], rest[STEPS:]
    panel = l_ref.shape[1]
    listed_count = y_ref.shape[1] // BLK

    @pl.when(pl.program_id(0) == 0)
    def _():
        for s in range(STEPS):
            high, low = split(y_ref[s])
            yh[s], yl[s] = high, low
            high, low = split(y_ref[s].T)
            yth[s], ytl[s] = high, low
            high, low = split(l_ref[s].T)
            lth[s], ltl[s] = high, low

    out_ref[...] = m_ref[...]
    for s in range(STEPS):
        starts = [pl.multiple_of(listed[s, k] * BLK, BLK) for k in range(listed_count)]
        gathered = jnp.concatenate([out_ref[pl.ds(start, BLK), :] for start in starts], axis=0)
        projected = product3((yth[s], ytl[s]), split(gathered), NN)
        update = product3((lth[s], ltl[s]), split(projected), NN)
        renewed = gathered - product3((yh[s], yl[s]), split(update), NN)
        for k, start in enumerate(starts):
            out_ref[pl.ds(start, BLK), :] = renewed[k * BLK : (k + 1) * BLK]
    for s in range(STEPS):
        turned = out_ref[s * panel : (s + 1) * panel, :].T
        tops_refs[s][...] = turned

        @pl.when(odd[s] == 1)
        def _():
            tops_refs[s][...] = product3(split(turned), split(u_ref[s]), NN)


def leaf(matrix, leaf_vectors, leaf_factors, tree_vectors, leaf_blocks, odd):
    rows, columns = matrix.shape
    width = COLS_PER_LEAF
    steps, leaf_rows, panel = leaf_vectors.shape
    return pl.pallas_call(
        leaf_kernel,
        out_shape=(
            jax.ShapeDtypeStruct((rows, columns), jnp.float32),
            *[jax.ShapeDtypeStruct((columns, panel), jnp.float32)] * steps,
        ),
        grid_spec=pltpu.PrefetchScalarGridSpec(
            num_scalar_prefetch=2,
            grid=(columns // width,),
            in_specs=[
                pl.BlockSpec((rows, width), lambda c, *_: (0, c)),
                pl.BlockSpec(leaf_vectors.shape, lambda c, *_: (0, 0, 0)),
                pl.BlockSpec(leaf_factors.shape, lambda c, *_: (0, 0, 0)),
                pl.BlockSpec(tree_vectors.shape, lambda c, *_: (0, 0, 0)),
            ],
            out_specs=[
                pl.BlockSpec((rows, width), lambda c, *_: (0, c)),
                *[pl.BlockSpec((width, panel), lambda c, *_: (c, 0))] * steps,
            ],
            scratch_shapes=[
                pltpu.VMEM((steps, leaf_rows, panel), jnp.bfloat16),
                pltpu.VMEM((steps, leaf_rows, panel), jnp.bfloat16),
                pltpu.VMEM((steps, panel, leaf_rows), jnp.bfloat16),
                pltpu.VMEM((steps, panel, leaf_rows), jnp.bfloat16),
                pltpu.VMEM((steps, panel, panel), jnp.bfloat16),
                pltpu.VMEM((steps, panel, panel), jnp.bfloat16),
            ],
        ),
    )(leaf_blocks, odd, matrix, leaf_vectors, leaf_factors, tree_vectors)


def corner_masks(half):
    row = lax.broadcasted_iota(jnp.int32, (half, half), 0)
    column = lax.broadcasted_iota(jnp.int32, (half, half), 1)
    return row < column, row == column


def pack_kernel(odd, own_ref, other_ref, f_ref, *out_refs):
    half = own_ref.shape[1]
    above, on = corner_masks(half)
    for s, out_ref in enumerate(out_refs):
        out_ref[:half, :] = own_ref[s]

        @pl.when(odd[s] == 1)
        def _():
            out_ref[:half, :] = other_ref[s]

        first = f_ref[s, :half, :half]
        second = f_ref[s, half:, half:]
        out_ref[half : 2 * half, :half] = jnp.where(above | on, first, second.T)
        out_ref[half : 2 * half, half:] = f_ref[s, :half, half:]
        diagonal = jnp.sum(jnp.where(on, second, 0.0), axis=0, keepdims=True)
        line = jnp.concatenate([diagonal, jnp.zeros_like(diagonal)], axis=1)
        out_ref[2 * half :, :] = jnp.broadcast_to(line, (8, 2 * half))


def pack(own, other, factors, odd):
    steps, half, panel = own.shape
    shape = (panel + 8, panel)
    return pl.pallas_call(
        pack_kernel,
        out_shape=[jax.ShapeDtypeStruct(shape, jnp.float32)] * steps,
        grid_spec=pltpu.PrefetchScalarGridSpec(
            num_scalar_prefetch=1,
            grid=(1,),
            in_specs=[
                pl.BlockSpec(own.shape, lambda c, *_: (0, 0, 0)),
                pl.BlockSpec(other.shape, lambda c, *_: (0, 0, 0)),
                pl.BlockSpec(factors.shape, lambda c, *_: (0, 0, 0)),
            ],
            out_specs=[pl.BlockSpec(shape, lambda c, *_: (0, 0))] * steps,
        ),
    )(odd, own, other, factors)


def tree_kernel(upper, lower, x_ref, g_ref, out_ref):
    node = pl.program_id(0)
    panel = g_ref.shape[2]
    half = panel // 2
    first_level = x_ref.shape[0] // 2

    @pl.when(node == 0)
    def _():
        out_ref[...] = x_ref[...]

    a, b = upper[node], lower[node]
    slot = lax.rem(b, 2)
    above, on = corner_masks(half)
    corner = g_ref[slot, half : 2 * half, :half]
    diagonal = g_ref[slot, 2 * half : 2 * half + 1, :half]
    top = jnp.concatenate(
        [jnp.where(above | on, corner, 0.0), g_ref[slot, half : 2 * half, half:]], axis=1
    )
    last = jnp.where(above, corner.T, jnp.where(on, diagonal, 0.0))
    bottom = jnp.concatenate([jnp.zeros_like(last), last], axis=1)
    f = split(jnp.concatenate([top, bottom], axis=0))
    xa, xb = out_ref[a], out_ref[b]

    @pl.when(node < first_level)
    def _():
        w = product3(split(xa + xb), f, NN)
        out_ref[a] = xa - w
        out_ref[b] = w

    @pl.when(node >= first_level)
    def _():
        u = split(jnp.concatenate([g_ref[0, :half, :], g_ref[1, :half, :]], axis=0))
        w = product3(split(xa + product3(split(xb), u, NN)), f, NN)
        out_ref[a] = xa - w
        out_ref[b] = xb - product3(split(w), u, NT)


def tree(spread, reflectors, upper, lower):
    devices = spread.shape[0]
    return pl.pallas_call(
        tree_kernel,
        out_shape=jax.ShapeDtypeStruct(spread.shape, jnp.float32),
        grid_spec=pltpu.PrefetchScalarGridSpec(
            num_scalar_prefetch=2,
            grid=(devices - 1,),
            in_specs=[
                pl.BlockSpec(spread.shape, lambda n, *_: (0, 0, 0)),
                pl.BlockSpec((2,) + reflectors.shape[1:], lambda n, up, lo: (lo[n] // 2, 0, 0)),
            ],
            out_specs=pl.BlockSpec(spread.shape, lambda n, *_: (0, 0, 0)),
        ),
    )(upper, lower, spread, reflectors)


def place_kernel(odd, back_ref, u_ref, work_ref, out_ref):
    @pl.when(odd[0] == 0)
    def _():
        out_ref[...] = back_ref[...].T

    @pl.when(odd[0] == 1)
    def _():
        out_ref[...] = work_ref[...] - product3(split(u_ref[...]), split(back_ref[...]), NT)


def place(step, back, vectors, work, odd):
    columns, panel = back.shape
    width = COLS_PER_LEAF
    return pl.pallas_call(
        place_kernel,
        out_shape=jax.ShapeDtypeStruct(work.shape, jnp.float32),
        grid_spec=pltpu.PrefetchScalarGridSpec(
            num_scalar_prefetch=1,
            grid=(columns // width,),
            in_specs=[
                pl.BlockSpec((width, panel), lambda c, *_: (c, 0)),
                pl.BlockSpec((panel, panel), lambda c, *_: (0, 0)),
                pl.BlockSpec((panel, width), lambda c, *_: (step, c)),
            ],
            out_specs=pl.BlockSpec((panel, width), lambda c, *_: (step, c)),
        ),
        input_output_aliases={3: 0},
    )(odd, back, vectors, work)


def pairs(row_count):
    uppers, lowers = [], []
    gap = 1
    while gap < row_count:
        for start in range(0, row_count, 2 * gap):
            uppers.append(start)
            lowers.append(start + gap)
        gap *= 2
    return jnp.array(uppers, jnp.int32), jnp.array(lowers, jnp.int32)


def shards(matrix, leaf_vectors, leaf_factors, tree_vectors, tree_factors, leaf_blocks, owner):
    row_count = lax.axis_size("row")
    my_index = lax.axis_index("row")
    columns = matrix.shape[1]
    panel = tree_vectors.shape[2]
    half = panel // 2
    core = my_index % 2
    odd = ((my_index - owner) % 2).astype(jnp.int32)
    own = lax.dynamic_slice_in_dim(tree_vectors, core * half, half, axis=1)
    asked = lax.dynamic_slice_in_dim(tree_vectors, (1 - core) * half, half, axis=1)
    other = lax.ppermute(asked, "row", [(i, i ^ 1) for i in range(row_count)])
    packed = pack(own, other, tree_factors, odd)
    reflectors = [lax.all_gather(p, "row") for p in packed]
    work, *tops = leaf(matrix, leaf_vectors, leaf_factors, tree_vectors, leaf_blocks, odd)
    uppers, lowers = pairs(row_count)
    for s in range(STEPS):
        spread = tops[s].reshape(row_count, columns // row_count, panel)
        spread = lax.all_to_all(spread, "row", 0, 0)
        upper, lower = (uppers + owner[s]) % row_count, (lowers + owner[s]) % row_count
        done = tree(spread, reflectors[s], upper, lower)
        back = lax.all_to_all(done, "row", 0, 0).reshape(columns, panel)
        work = place(s, back, tree_vectors[s], work, odd[s : s + 1])
    return work


def solution(mesh):
    return jax.shard_map(
        shards,
        mesh=mesh,
        in_specs=(
            P(("groups", "row"), None),
            P("groups", "row", None),
            P("groups", "row", None),
            P("groups", "row", None),
            P("groups", "row", None),
            P("groups", "row"),
            P("groups"),
        ),
        out_specs=P(("groups", "row"), None),
        check_vma=False,
    )
```

```python
import functools

import jax
import jax.numpy as jnp
from jax import lax
from jax.experimental import pallas as pl
from jax.experimental.pallas import tpu as pltpu
from jax.sharding import PartitionSpec as P

BLK = 128
STEPS = 2
COLS_PER_LEAF = 256

NN = (((1,), (0,)), ((), ()))
TN = (((0,), (0,)), ((), ()))
NT = (((1,), (1,)), ((), ()))


def split(value):
    high = value.astype(jnp.bfloat16)
    low = (value - high.astype(jnp.float32)).astype(jnp.bfloat16)
    return high, low


def product3(left, right, dims):
    def one(a, b):
        return lax.dot_general(a, b, dims, preferred_element_type=jnp.float32)

    return one(left[0], right[0]) + (one(left[0], right[1]) + one(left[1], right[0]))


def leaf_kernel(listed, odd, m_ref, y_ref, l_ref, u_ref, out_ref, tops_ref, yh, yl, yth, ytl, lth, ltl):
    panel = l_ref.shape[1]
    listed_count = y_ref.shape[1] // BLK

    @pl.when(pl.program_id(0) == 0)
    def _():
        for s in range(STEPS):
            high, low = split(y_ref[s])
            yh[s], yl[s] = high, low
            high, low = split(y_ref[s].T)
            yth[s], ytl[s] = high, low
            high, low = split(l_ref[s].T)
            lth[s], ltl[s] = high, low

    out_ref[...] = m_ref[...]
    for s in range(STEPS):
        starts = [pl.multiple_of(listed[s, k] * BLK, BLK) for k in range(listed_count)]
        gathered = jnp.concatenate([out_ref[pl.ds(start, BLK), :] for start in starts], axis=0)
        projected = product3((yth[s], ytl[s]), split(gathered), NN)
        update = product3((lth[s], ltl[s]), split(projected), NN)
        renewed = gathered - product3((yh[s], yl[s]), split(update), NN)
        for k, start in enumerate(starts):
            out_ref[pl.ds(start, BLK), :] = renewed[k * BLK : (k + 1) * BLK]
    for s in range(STEPS):
        turned = out_ref[s * panel : (s + 1) * panel, :].T
        place_here = slice(s * panel, (s + 1) * panel)
        tops_ref[:, place_here] = turned

        @pl.when(odd[s] == 1)
        def _():
            tops_ref[:, place_here] = product3(split(turned), split(u_ref[s]), NN)


def leaf(matrix, leaf_vectors, leaf_factors, tree_vectors, leaf_blocks, odd):
    rows, columns = matrix.shape
    width = COLS_PER_LEAF
    steps, leaf_rows, panel = leaf_vectors.shape
    return pl.pallas_call(
        leaf_kernel,
        out_shape=(
            jax.ShapeDtypeStruct((rows, columns), jnp.float32),
            jax.ShapeDtypeStruct((columns, steps * panel), jnp.float32),
        ),
        grid_spec=pltpu.PrefetchScalarGridSpec(
            num_scalar_prefetch=2,
            grid=(columns // width,),
            in_specs=[
                pl.BlockSpec((rows, width), lambda c, *_: (0, c)),
                pl.BlockSpec(leaf_vectors.shape, lambda c, *_: (0, 0, 0)),
                pl.BlockSpec(leaf_factors.shape, lambda c, *_: (0, 0, 0)),
                pl.BlockSpec(tree_vectors.shape, lambda c, *_: (0, 0, 0)),
            ],
            out_specs=[
                pl.BlockSpec((rows, width), lambda c, *_: (0, c)),
                pl.BlockSpec((width, steps * panel), lambda c, *_: (c, 0)),
            ],
            scratch_shapes=[
                pltpu.VMEM((steps, leaf_rows, panel), jnp.bfloat16),
                pltpu.VMEM((steps, leaf_rows, panel), jnp.bfloat16),
                pltpu.VMEM((steps, panel, leaf_rows), jnp.bfloat16),
                pltpu.VMEM((steps, panel, leaf_rows), jnp.bfloat16),
                pltpu.VMEM((steps, panel, panel), jnp.bfloat16),
                pltpu.VMEM((steps, panel, panel), jnp.bfloat16),
            ],
        ),
    )(leaf_blocks, odd, matrix, leaf_vectors, leaf_factors, tree_vectors)


def corner_masks(half):
    row = lax.broadcasted_iota(jnp.int32, (half, half), 0)
    column = lax.broadcasted_iota(jnp.int32, (half, half), 1)
    return row < column, row == column


def pack_kernel(odd, own_ref, other_ref, f_ref, all_ref):
    half = own_ref.shape[1]
    above, on = corner_masks(half)
    for s in range(STEPS):
        out_ref = all_ref.at[s]
        out_ref[:half, :] = own_ref[s]

        @pl.when(odd[s] == 1)
        def _():
            out_ref[:half, :] = other_ref[s]

        first = f_ref[s, :half, :half]
        second = f_ref[s, half:, half:]
        out_ref[half : 2 * half, :half] = jnp.where(above | on, first, second.T)
        out_ref[half : 2 * half, half:] = f_ref[s, :half, half:]
        diagonal = jnp.sum(jnp.where(on, second, 0.0), axis=0, keepdims=True)
        line = jnp.concatenate([diagonal, jnp.zeros_like(diagonal)], axis=1)
        out_ref[2 * half :, :] = jnp.broadcast_to(line, (8, 2 * half))


def pack(own, other, factors, odd):
    steps, half, panel = own.shape
    shape = (steps, panel + 8, panel)
    return pl.pallas_call(
        pack_kernel,
        out_shape=jax.ShapeDtypeStruct(shape, jnp.float32),
        grid_spec=pltpu.PrefetchScalarGridSpec(
            num_scalar_prefetch=1,
            grid=(1,),
            in_specs=[
                pl.BlockSpec(own.shape, lambda c, *_: (0, 0, 0)),
                pl.BlockSpec(other.shape, lambda c, *_: (0, 0, 0)),
                pl.BlockSpec(factors.shape, lambda c, *_: (0, 0, 0)),
            ],
            out_specs=pl.BlockSpec(shape, lambda c, *_: (0, 0, 0)),
        ),
    )(odd, own, other, factors)


def chip_at(place, chips):
    return jnp.where(place < chips // 2, 2 * place, 2 * (chips - 1 - place) + 1)


def place_of(chip, chips):
    return jnp.where(chip % 2 == 0, chip // 2, chips - 1 - chip // 2)


def exchange_kernel(
    count, p_ref, t_ref, g_ref, r_ref, ring_send, ring_recv, pass_send, pass_recv, a2a_send, a2a_recv, own_sem
):
    me = lax.axis_index("row")
    chips = count // 2
    core = me % 2
    place = place_of(me // 2, chips)

    def device(offset):
        return chip_at((place + offset + chips) % chips, chips) * 2 + core

    partner = me + 1 - 2 * core
    right, left = device(1), device(-1)

    barrier = pltpu.get_barrier_semaphore()
    for j in range(1, count):
        pl.semaphore_signal(
            barrier, inc=1, device_id={"row": (me + j) % count}, device_id_type=pl.DeviceIdType.MESH
        )
    pl.semaphore_wait(barrier, count - 1)

    def send(source, target, send_sem, recv_sem, peer):
        return pltpu.make_async_remote_copy(
            src_ref=source,
            dst_ref=target,
            send_sem=send_sem,
            recv_sem=recv_sem,
            device_id={"row": peer},
            device_id_type=pl.DeviceIdType.MESH,
        )

    lengths = {(0, 0): chips // 2, (0, 1): chips - 1 - chips // 2}
    lengths[1, 1], lengths[1, 0] = lengths[0, 0], lengths[0, 1]
    waits = []

    def hop(s, way, t):
        origin = device(-t if way == 0 else t)
        source = p_ref.at[s] if t == 0 else g_ref.at[origin, s]
        copy = send(
            source,
            g_ref.at[origin, s],
            ring_send.at[s, way, t],
            ring_recv.at[s, way, t],
            right if way == 0 else left,
        )
        copy.start()
        waits.append(copy.wait_send)
        return copy

    def hand(s, slot, source, origin):
        copy = send(source, g_ref.at[origin, s], pass_send.at[s, slot], pass_recv.at[s, slot], partner)
        copy.start()
        waits.append(copy.wait)

    def scatter(j):
        peer = (me + j) % count
        copy = send(t_ref.at[peer], r_ref.at[me], a2a_send.at[j - 1], a2a_recv.at[j - 1], peer)
        copy.start()
        waits.append(copy.wait)

    flying = {}
    for s, way in lengths:
        if lengths[s, way] > 0:
            flying[s, way] = hop(s, way, 0)
    for s in range(STEPS):
        hand(s, 0, p_ref.at[s], me)
        copy = pltpu.make_async_copy(p_ref.at[s], g_ref.at[me, s], own_sem.at[s])
        copy.start()
        waits.append(copy.wait)
    copy = pltpu.make_async_copy(t_ref.at[me], r_ref.at[me], own_sem.at[STEPS])
    copy.start()
    waits.append(copy.wait)

    longest = max(lengths.values())
    todo = [(j + count // 2 - 1) % (count - 1) + 1 for j in range(count - 1)]
    share = -(-len(todo) // longest)
    for t in range(longest):
        for j in todo[t * share : (t + 1) * share]:
            scatter(j)
        for s, way in lengths:
            if t < lengths[s, way]:
                flying[s, way].wait_recv()
                origin = device(-t - 1 if way == 0 else t + 1)
                if t + 1 < lengths[s, way]:
                    flying[s, way] = hop(s, way, t + 1)
                slot = 1 + (t if way == 0 else lengths[s, 0] + t)
                hand(s, slot, g_ref.at[origin, s], origin)
    for wait in waits:
        wait()


def exchange(packed, spread):
    count = spread.shape[0]
    chips = count // 2
    dma = pltpu.SemaphoreType.DMA
    return pl.pallas_call(
        functools.partial(exchange_kernel, count),
        out_shape=(
            jax.ShapeDtypeStruct((count,) + packed.shape, jnp.float32),
            jax.ShapeDtypeStruct(spread.shape, jnp.float32),
        ),
        in_specs=[pl.BlockSpec(memory_space=pltpu.VMEM), pl.BlockSpec(memory_space=pl.ANY)],
        out_specs=[pl.BlockSpec(memory_space=pl.ANY)] * 2,
        scratch_shapes=[
            dma((STEPS, 2, chips)),
            dma((STEPS, 2, chips)),
            dma((STEPS, chips)),
            dma((STEPS, chips)),
            dma((count - 1,)),
            dma((count - 1,)),
            dma((STEPS + 1,)),
        ],
        compiler_params=pltpu.CompilerParams(collective_id=0, has_side_effects=True),
    )(packed, spread)


def tree_kernel(upper, lower, x_ref, g_ref, out_ref):
    node = pl.program_id(0)
    panel = g_ref.shape[2]
    half = panel // 2
    first_level = x_ref.shape[0] // 2

    @pl.when(node == 0)
    def _():
        out_ref[...] = x_ref[...]

    a, b = upper[node], lower[node]
    slot = lax.rem(b, 2)
    above, on = corner_masks(half)
    corner = g_ref[slot, half : 2 * half, :half]
    diagonal = g_ref[slot, 2 * half : 2 * half + 1, :half]
    top = jnp.concatenate(
        [jnp.where(above | on, corner, 0.0), g_ref[slot, half : 2 * half, half:]], axis=1
    )
    last = jnp.where(above, corner.T, jnp.where(on, diagonal, 0.0))
    bottom = jnp.concatenate([jnp.zeros_like(last), last], axis=1)
    f = split(jnp.concatenate([top, bottom], axis=0))
    xa, xb = out_ref[a], out_ref[b]

    @pl.when(node < first_level)
    def _():
        w = product3(split(xa + xb), f, NN)
        out_ref[a] = xa - w
        out_ref[b] = w

    @pl.when(node >= first_level)
    def _():
        u = split(jnp.concatenate([g_ref[0, :half, :], g_ref[1, :half, :]], axis=0))
        w = product3(split(xa + product3(split(xb), u, NN)), f, NN)
        out_ref[a] = xa - w
        out_ref[b] = xb - product3(split(w), u, NT)


def tree(step, spread, reflectors, upper, lower):
    devices, width, both = spread.shape
    block = (devices, width, both // STEPS)
    return pl.pallas_call(
        tree_kernel,
        out_shape=jax.ShapeDtypeStruct(block, jnp.float32),
        grid_spec=pltpu.PrefetchScalarGridSpec(
            num_scalar_prefetch=2,
            grid=(devices - 1,),
            in_specs=[
                pl.BlockSpec(block, lambda n, *_: (0, 0, step)),
                pl.BlockSpec(
                    (2, None) + reflectors.shape[2:], lambda n, up, lo: (lo[n] // 2, step, 0, 0)
                ),
            ],
            out_specs=pl.BlockSpec(block, lambda n, *_: (0, 0, 0)),
        ),
    )(upper, lower, spread, reflectors)


def place_kernel(odd, back_ref, u_ref, work_ref, out_ref):
    @pl.when(odd[0] == 0)
    def _():
        out_ref[...] = back_ref[...].T

    @pl.when(odd[0] == 1)
    def _():
        out_ref[...] = work_ref[...] - product3(split(u_ref[...]), split(back_ref[...]), NT)


def place(step, back, vectors, work, odd):
    columns, panel = back.shape
    width = COLS_PER_LEAF
    return pl.pallas_call(
        place_kernel,
        out_shape=jax.ShapeDtypeStruct(work.shape, jnp.float32),
        grid_spec=pltpu.PrefetchScalarGridSpec(
            num_scalar_prefetch=1,
            grid=(columns // width,),
            in_specs=[
                pl.BlockSpec((width, panel), lambda c, *_: (c, 0)),
                pl.BlockSpec((panel, panel), lambda c, *_: (0, 0)),
                pl.BlockSpec((panel, width), lambda c, *_: (step, c)),
            ],
            out_specs=pl.BlockSpec((panel, width), lambda c, *_: (step, c)),
        ),
        input_output_aliases={3: 0},
    )(odd, back, vectors, work)


def pairs(row_count):
    uppers, lowers = [], []
    gap = 1
    while gap < row_count:
        for start in range(0, row_count, 2 * gap):
            uppers.append(start)
            lowers.append(start + gap)
        gap *= 2
    return jnp.array(uppers, jnp.int32), jnp.array(lowers, jnp.int32)


def shards(matrix, leaf_vectors, leaf_factors, tree_vectors, tree_factors, leaf_blocks, owner):
    row_count = lax.axis_size("row")
    my_index = lax.axis_index("row")
    columns = matrix.shape[1]
    panel = tree_vectors.shape[2]
    half = panel // 2
    core = my_index % 2
    odd = ((my_index - owner) % 2).astype(jnp.int32)
    own = lax.dynamic_slice_in_dim(tree_vectors, core * half, half, axis=1)
    asked = lax.dynamic_slice_in_dim(tree_vectors, (1 - core) * half, half, axis=1)
    other = lax.ppermute(asked, "row", [(i, i ^ 1) for i in range(row_count)])
    packed = pack(own, other, tree_factors, odd)
    work, tops = leaf(matrix, leaf_vectors, leaf_factors, tree_vectors, leaf_blocks, odd)
    reflectors, spread = exchange(
        packed, tops.reshape(row_count, columns // row_count, STEPS * panel)
    )
    uppers, lowers = pairs(row_count)
    for s in range(STEPS):
        upper, lower = (uppers + owner[s]) % row_count, (lowers + owner[s]) % row_count
        done = tree(s, spread, reflectors, upper, lower)
        back = lax.all_to_all(done, "row", 0, 0).reshape(columns, panel)
        work = place(s, back, tree_vectors[s], work, odd[s : s + 1])
    return work


def solution(mesh):
    return jax.shard_map(
        shards,
        mesh=mesh,
        in_specs=(
            P(("groups", "row"), None),
            P("groups", "row", None),
            P("groups", "row", None),
            P("groups", "row", None),
            P("groups", "row", None),
            P("groups", "row"),
            P("groups"),
        ),
        out_specs=P(("groups", "row"), None),
        check_vma=False,
    )
```

```python
import functools

import jax
import jax.numpy as jnp
from jax import lax
from jax.experimental import pallas as pl
from jax.experimental.pallas import tpu as pltpu
from jax.sharding import PartitionSpec as P

BLK = 128
STEPS = 2
COLS_PER_LEAF = 256

NN = (((1,), (0,)), ((), ()))
TN = (((0,), (0,)), ((), ()))
NT = (((1,), (1,)), ((), ()))


def split(value):
    high = value.astype(jnp.bfloat16)
    low = (value - high.astype(jnp.float32)).astype(jnp.bfloat16)
    return high, low


def product3(left, right, dims):
    def one(a, b):
        return lax.dot_general(a, b, dims, preferred_element_type=jnp.float32)

    return one(left[0], right[0]) + (one(left[0], right[1]) + one(left[1], right[0]))


def corner_masks(half):
    row = lax.broadcasted_iota(jnp.int32, (half, half), 0)
    column = lax.broadcasted_iota(jnp.int32, (half, half), 1)
    return row < column, row == column


def pack_kernel(odd, own_ref, other_ref, f_ref, all_ref):
    half = own_ref.shape[1]
    above, on = corner_masks(half)
    for s in range(STEPS):
        out_ref = all_ref.at[s]
        out_ref[:half, :] = own_ref[s]

        @pl.when(odd[s] == 1)
        def _():
            out_ref[:half, :] = other_ref[s]

        first = f_ref[s, :half, :half]
        second = f_ref[s, half:, half:]
        out_ref[half : 2 * half, :half] = jnp.where(above | on, first, second.T)
        out_ref[half : 2 * half, half:] = f_ref[s, :half, half:]
        diagonal = jnp.sum(jnp.where(on, second, 0.0), axis=0, keepdims=True)
        line = jnp.concatenate([diagonal, jnp.zeros_like(diagonal)], axis=1)
        out_ref[2 * half :, :] = jnp.broadcast_to(line, (8, 2 * half))


def pack(own, other, factors, odd):
    steps, half, panel = own.shape
    shape = (steps, panel + 8, panel)
    return pl.pallas_call(
        pack_kernel,
        out_shape=jax.ShapeDtypeStruct(shape, jnp.float32),
        grid_spec=pltpu.PrefetchScalarGridSpec(
            num_scalar_prefetch=1,
            grid=(1,),
            in_specs=[
                pl.BlockSpec(own.shape, lambda c, *_: (0, 0, 0)),
                pl.BlockSpec(other.shape, lambda c, *_: (0, 0, 0)),
                pl.BlockSpec(factors.shape, lambda c, *_: (0, 0, 0)),
            ],
            out_specs=pl.BlockSpec(shape, lambda c, *_: (0, 0, 0)),
        ),
    )(odd, own, other, factors)


def chip_at(place, chips):
    return jnp.where(place < chips // 2, 2 * place, 2 * (chips - 1 - place) + 1)


def place_of(chip, chips):
    return jnp.where(chip % 2 == 0, chip // 2, chips - 1 - chip // 2)


def leaf_block(listed, odd, m_ref, u_ref, out_ref, tops_ref, first, parts):
    yh, yl, yth, ytl, lth, ltl, uh, ul = parts
    panel = u_ref.shape[1]
    width = out_ref.shape[1]
    block_count = out_ref.shape[0] // BLK
    listed_count = yh.shape[1] // BLK
    panel_blocks = panel // BLK
    out_ref[...] = m_ref[...]
    for s in range(STEPS):
        inner = range((s + 1) * panel_blocks, block_count - 1)
        numbers = {
            k: jnp.full((BLK, width), listed[s, k], jnp.int32)
            for k in range(panel_blocks, listed_count - 1)
        }
        taken = [out_ref[s * panel : (s + 1) * panel, :]]
        for number in numbers.values():
            block_rows = jnp.zeros((BLK, width), jnp.float32)
            for block in inner:
                here = out_ref[block * BLK : (block + 1) * BLK, :]
                block_rows = jnp.where(number == block, here, block_rows)
            taken.append(block_rows)
        taken.append(out_ref[(block_count - 1) * BLK :, :])
        gathered = jnp.concatenate(taken, axis=0)
        projected = product3((yth[s], ytl[s]), split(gathered), NN)
        update = product3((lth[s], ltl[s]), split(projected), NN)
        change = product3((yh[s], yl[s]), split(update), NN)
        pieces = [change[k * BLK : (k + 1) * BLK] for k in range(listed_count)]
        fixed = [(s * panel_blocks + k, pieces[k]) for k in range(panel_blocks)]
        for block, piece in fixed + [(block_count - 1, pieces[-1])]:
            out_ref[block * BLK : (block + 1) * BLK, :] -= piece
        for block in inner:
            amount = jnp.zeros((BLK, width), jnp.float32)
            for k, number in numbers.items():
                amount = jnp.where(number == block, pieces[k], amount)
            out_ref[block * BLK : (block + 1) * BLK, :] -= amount
    for s in range(STEPS):
        turned = out_ref[s * panel : (s + 1) * panel, :].T
        projected = product3(split(turned), (uh[s], ul[s]), NN)
        flag = jnp.full(turned.shape, odd[s], jnp.int32)
        tops_ref[pl.ds(first, width), s * panel : (s + 1) * panel] = jnp.where(
            flag == 1, projected, turned
        )


def exchange_kernel(count, listed, odd, m_ref, y_ref, l_ref, u_ref, p_ref, work_ref, g_ref, r_ref, *rest):
    parts = rest[:8]
    t_ref, ring_send, ring_recv, pass_send, pass_recv, a2a_send, a2a_recv, own_sem = rest[8:]
    turn = pl.program_id(0)
    turns = t_ref.shape[0] // m_ref.shape[1]
    me = lax.axis_index("row")
    chips = count // 2
    share = t_ref.shape[0] // count
    core = me % 2
    place = place_of(me // 2, chips)

    def device(offset):
        return chip_at((place + offset + chips) % chips, chips) * 2 + core

    partner = me + 1 - 2 * core
    right, left = device(1), device(-1)

    def remote(source, target, send_sem, recv_sem, peer):
        return pltpu.make_async_remote_copy(
            src_ref=source,
            dst_ref=target,
            send_sem=send_sem,
            recv_sem=recv_sem,
            device_id={"row": peer},
            device_id_type=pl.DeviceIdType.MESH,
        )

    lengths = {(0, 0): chips // 2, (0, 1): chips - 1 - chips // 2}
    lengths[1, 1], lengths[1, 0] = lengths[0, 0], lengths[0, 1]
    longest = max(lengths.values())

    def hop(s, way, t):
        origin = device(-t if way == 0 else t)
        source = p_ref.at[s] if t == 0 else g_ref.at[origin, s]
        return remote(
            source,
            g_ref.at[origin, s],
            ring_send.at[s, way, t],
            ring_recv.at[s, way, t],
            right if way == 0 else left,
        )

    def hand(s, way, t):
        if t < 0:
            return remote(
                p_ref.at[s], g_ref.at[me, s], pass_send.at[s, 0], pass_recv.at[s, 0], partner
            )
        origin = device(-t - 1 if way == 0 else t + 1)
        slot = 1 + (t if way == 0 else lengths[s, 0] + t)
        piece = g_ref.at[origin, s]
        return remote(piece, piece, pass_send.at[s, slot], pass_recv.at[s, slot], partner)

    def columns_of(peer):
        return t_ref.at[pl.ds(pl.multiple_of(peer * share, 8), share), :]

    def scatter(j):
        peer = (me + j) % count
        return remote(columns_of(peer), r_ref.at[me], a2a_send.at[j - 1], a2a_recv.at[j - 1], peer)

    def keep(s):
        return pltpu.make_async_copy(p_ref.at[s], g_ref.at[me, s], own_sem.at[s])

    def keep_columns():
        return pltpu.make_async_copy(columns_of(me), r_ref.at[me], own_sem.at[STEPS])

    def advance(t):
        for s, way in lengths:
            if t < lengths[s, way]:
                hop(s, way, t).wait_recv()
                if t + 1 < lengths[s, way]:
                    hop(s, way, t + 1).start()
                hand(s, way, t).start()

    @pl.when(turn == 0)
    def _():
        barrier = pltpu.get_barrier_semaphore()
        for j in range(1, count):
            pl.semaphore_signal(
                barrier,
                inc=1,
                device_id={"row": (me + j) % count},
                device_id_type=pl.DeviceIdType.MESH,
            )
        pl.semaphore_wait(barrier, count - 1)
        for s, way in lengths:
            if lengths[s, way] > 0:
                hop(s, way, 0).start()
        for s in range(STEPS):
            hand(s, 0, -1).start()
            keep(s).start()
        yh, yl, yth, ytl, lth, ltl, uh, ul = parts
        for s in range(STEPS):
            yh[s], yl[s] = split(y_ref[s])
            yth[s], ytl[s] = split(y_ref[s].T)
            lth[s], ltl[s] = split(l_ref[s].T)
            uh[s], ul[s] = split(u_ref[s])

    first = pl.multiple_of(turn * m_ref.shape[1], m_ref.shape[1])
    leaf_block(listed, odd, m_ref, u_ref, work_ref, t_ref, first, parts)

    early = min(turns - 1, longest)
    for t in range(early):

        @pl.when(turn == t)
        def _():
            advance(t)

    @pl.when(turn == turns - 1)
    def _():
        todo = [(j + count // 2 - 1) % (count - 1) + 1 for j in range(count - 1)]
        rounds = max(longest - early, 1)
        size = -(-len(todo) // rounds)
        keep_columns().start()
        for t in range(rounds):
            for j in todo[t * size : (t + 1) * size]:
                scatter(j).start()
            advance(early + t)
        for s, way in lengths:
            for t in range(lengths[s, way]):
                hop(s, way, t).wait_send()
                hand(s, way, t).wait()
        for s in range(STEPS):
            hand(s, 0, -1).wait()
            keep(s).wait()
        keep_columns().wait()
        for j in todo:
            scatter(j).wait()


def exchange(count, matrix, leaf_vectors, leaf_factors, tree_vectors, packed, leaf_blocks, odd):
    rows, columns = matrix.shape
    width = COLS_PER_LEAF
    steps, leaf_rows, panel = leaf_vectors.shape
    chips = count // 2
    dma = pltpu.SemaphoreType.DMA
    half_type = jnp.bfloat16

    def whole(array):
        return pl.BlockSpec(array.shape, lambda c, *_: (0, 0, 0))

    return pl.pallas_call(
        functools.partial(exchange_kernel, count),
        out_shape=(
            jax.ShapeDtypeStruct((rows, columns), jnp.float32),
            jax.ShapeDtypeStruct((count,) + packed.shape, jnp.float32),
            jax.ShapeDtypeStruct((count, columns // count, steps * panel), jnp.float32),
        ),
        grid_spec=pltpu.PrefetchScalarGridSpec(
            num_scalar_prefetch=2,
            grid=(columns // width,),
            in_specs=[
                pl.BlockSpec((rows, width), lambda c, *_: (0, c)),
                whole(leaf_vectors),
                whole(leaf_factors),
                whole(tree_vectors),
                whole(packed),
            ],
            out_specs=[
                pl.BlockSpec((rows, width), lambda c, *_: (0, c)),
                pl.BlockSpec(memory_space=pl.ANY),
                pl.BlockSpec(memory_space=pl.ANY),
            ],
            scratch_shapes=[
                *[pltpu.VMEM((steps, leaf_rows, panel), half_type)] * 2,
                *[pltpu.VMEM((steps, panel, leaf_rows), half_type)] * 2,
                *[pltpu.VMEM((steps, panel, panel), half_type)] * 4,
                pltpu.VMEM((columns, steps * panel), jnp.float32),
                dma((steps, 2, chips)),
                dma((steps, 2, chips)),
                dma((steps, chips)),
                dma((steps, chips)),
                dma((count - 1,)),
                dma((count - 1,)),
                dma((steps + 1,)),
            ],
        ),
        compiler_params=pltpu.CompilerParams(collective_id=0, has_side_effects=True),
    )(leaf_blocks, odd, matrix, leaf_vectors, leaf_factors, tree_vectors, packed)


def tree_kernel(upper, lower, x_ref, g_ref, out_ref):
    node = pl.program_id(0)
    panel = g_ref.shape[2]
    half = panel // 2
    first_level = x_ref.shape[0] // 2

    @pl.when(node == 0)
    def _():
        out_ref[...] = x_ref[...]

    a, b = upper[node], lower[node]
    slot = lax.rem(b, 2)
    above, on = corner_masks(half)
    corner = g_ref[slot, half : 2 * half, :half]
    diagonal = g_ref[slot, 2 * half : 2 * half + 1, :half]
    top = jnp.concatenate(
        [jnp.where(above | on, corner, 0.0), g_ref[slot, half : 2 * half, half:]], axis=1
    )
    last = jnp.where(above, corner.T, jnp.where(on, diagonal, 0.0))
    bottom = jnp.concatenate([jnp.zeros_like(last), last], axis=1)
    f = split(jnp.concatenate([top, bottom], axis=0))
    xa, xb = out_ref[a], out_ref[b]

    @pl.when(node < first_level)
    def _():
        w = product3(split(xa + xb), f, NN)
        out_ref[a] = xa - w
        out_ref[b] = w

    @pl.when(node >= first_level)
    def _():
        u = split(jnp.concatenate([g_ref[0, :half, :], g_ref[1, :half, :]], axis=0))
        w = product3(split(xa + product3(split(xb), u, NN)), f, NN)
        out_ref[a] = xa - w
        out_ref[b] = xb - product3(split(w), u, NT)


def tree(step, spread, reflectors, upper, lower):
    devices, width, both = spread.shape
    block = (devices, width, both // STEPS)
    return pl.pallas_call(
        tree_kernel,
        out_shape=jax.ShapeDtypeStruct(block, jnp.float32),
        grid_spec=pltpu.PrefetchScalarGridSpec(
            num_scalar_prefetch=2,
            grid=(devices - 1,),
            in_specs=[
                pl.BlockSpec(block, lambda n, *_: (0, 0, step)),
                pl.BlockSpec(
                    (2, None) + reflectors.shape[2:], lambda n, up, lo: (lo[n] // 2, step, 0, 0)
                ),
            ],
            out_specs=pl.BlockSpec(block, lambda n, *_: (0, 0, 0)),
        ),
    )(upper, lower, spread, reflectors)


def place_kernel(odd, back_ref, u_ref, work_ref, out_ref):
    @pl.when(odd[0] == 0)
    def _():
        out_ref[...] = back_ref[...].T

    @pl.when(odd[0] == 1)
    def _():
        out_ref[...] = work_ref[...] - product3(split(u_ref[...]), split(back_ref[...]), NT)


def place(step, back, vectors, work, odd):
    columns, panel = back.shape
    width = COLS_PER_LEAF
    return pl.pallas_call(
        place_kernel,
        out_shape=jax.ShapeDtypeStruct(work.shape, jnp.float32),
        grid_spec=pltpu.PrefetchScalarGridSpec(
            num_scalar_prefetch=1,
            grid=(columns // width,),
            in_specs=[
                pl.BlockSpec((width, panel), lambda c, *_: (c, 0)),
                pl.BlockSpec((panel, panel), lambda c, *_: (0, 0)),
                pl.BlockSpec((panel, width), lambda c, *_: (step, c)),
            ],
            out_specs=pl.BlockSpec((panel, width), lambda c, *_: (step, c)),
        ),
        input_output_aliases={3: 0},
    )(odd, back, vectors, work)


def pairs(row_count):
    uppers, lowers = [], []
    gap = 1
    while gap < row_count:
        for start in range(0, row_count, 2 * gap):
            uppers.append(start)
            lowers.append(start + gap)
        gap *= 2
    return jnp.array(uppers, jnp.int32), jnp.array(lowers, jnp.int32)


def shards(matrix, leaf_vectors, leaf_factors, tree_vectors, tree_factors, leaf_blocks, owner):
    row_count = lax.axis_size("row")
    my_index = lax.axis_index("row")
    columns = matrix.shape[1]
    panel = tree_vectors.shape[2]
    half = panel // 2
    core = my_index % 2
    odd = ((my_index - owner) % 2).astype(jnp.int32)
    own = lax.dynamic_slice_in_dim(tree_vectors, core * half, half, axis=1)
    asked = lax.dynamic_slice_in_dim(tree_vectors, (1 - core) * half, half, axis=1)
    other = lax.ppermute(asked, "row", [(i, i ^ 1) for i in range(row_count)])
    packed = pack(own, other, tree_factors, odd)
    work, reflectors, spread = exchange(
        row_count, matrix, leaf_vectors, leaf_factors, tree_vectors, packed, leaf_blocks, odd
    )
    uppers, lowers = pairs(row_count)
    for s in range(STEPS):
        upper, lower = (uppers + owner[s]) % row_count, (lowers + owner[s]) % row_count
        done = tree(s, spread, reflectors, upper, lower)
        back = lax.all_to_all(done, "row", 0, 0).reshape(columns, panel)
        work = place(s, back, tree_vectors[s], work, odd[s : s + 1])
    return work


def solution(mesh):
    return jax.shard_map(
        shards,
        mesh=mesh,
        in_specs=(
            P(("groups", "row"), None),
            P("groups", "row", None),
            P("groups", "row", None),
            P("groups", "row", None),
            P("groups", "row", None),
            P("groups", "row"),
            P("groups"),
        ),
        out_specs=P(("groups", "row"), None),
        check_vma=False,
    )
```

```python
import functools

import jax
import jax.numpy as jnp
from jax import lax
from jax.experimental import pallas as pl
from jax.experimental.pallas import tpu as pltpu
from jax.sharding import PartitionSpec as P

BLK = 128
STEPS = 2
COLS_PER_LEAF = 256

NN = (((1,), (0,)), ((), ()))
TN = (((0,), (0,)), ((), ()))
NT = (((1,), (1,)), ((), ()))


def split(value):
    high = value.astype(jnp.bfloat16)
    low = (value - high.astype(jnp.float32)).astype(jnp.bfloat16)
    return high, low


def product3(left, right, dims):
    def one(a, b):
        return lax.dot_general(a, b, dims, preferred_element_type=jnp.float32)

    return one(left[0], right[0]) + (one(left[0], right[1]) + one(left[1], right[0]))


def corner_masks(half):
    row = lax.broadcasted_iota(jnp.int32, (half, half), 0)
    column = lax.broadcasted_iota(jnp.int32, (half, half), 1)
    return row < column, row == column


def pack_kernel(odd, own_ref, other_ref, f_ref, all_ref):
    half = own_ref.shape[1]
    above, on = corner_masks(half)
    for s in range(STEPS):
        out_ref = all_ref.at[s]
        out_ref[:half, :] = own_ref[s]

        @pl.when(odd[s] == 1)
        def _():
            out_ref[:half, :] = other_ref[s]

        first = f_ref[s, :half, :half]
        second = f_ref[s, half:, half:]
        out_ref[half : 2 * half, :half] = jnp.where(above | on, first, second.T)
        out_ref[half : 2 * half, half:] = f_ref[s, :half, half:]
        diagonal = jnp.sum(jnp.where(on, second, 0.0), axis=0, keepdims=True)
        line = jnp.concatenate([diagonal, jnp.zeros_like(diagonal)], axis=1)
        out_ref[2 * half :, :] = jnp.broadcast_to(line, (8, 2 * half))


def pack(own, other, factors, odd):
    steps, half, panel = own.shape
    shape = (steps, panel + 8, panel)
    return pl.pallas_call(
        pack_kernel,
        out_shape=jax.ShapeDtypeStruct(shape, jnp.float32),
        grid_spec=pltpu.PrefetchScalarGridSpec(
            num_scalar_prefetch=1,
            grid=(1,),
            in_specs=[
                pl.BlockSpec(own.shape, lambda c, *_: (0, 0, 0)),
                pl.BlockSpec(other.shape, lambda c, *_: (0, 0, 0)),
                pl.BlockSpec(factors.shape, lambda c, *_: (0, 0, 0)),
            ],
            out_specs=pl.BlockSpec(shape, lambda c, *_: (0, 0, 0)),
        ),
    )(odd, own, other, factors)


def leaf_block(listed, odd, m_ref, u_ref, out_ref, tops_ref, first, parts):
    yh, yl, yth, ytl, lth, ltl, uh, ul = parts
    panel = u_ref.shape[1]
    width = out_ref.shape[1]
    block_count = out_ref.shape[0] // BLK
    listed_count = yh.shape[1] // BLK
    panel_blocks = panel // BLK
    out_ref[...] = m_ref[...]
    for s in range(STEPS):
        inner = range((s + 1) * panel_blocks, block_count - 1)
        numbers = {
            k: jnp.full((BLK, width), listed[s, k], jnp.int32)
            for k in range(panel_blocks, listed_count - 1)
        }
        taken = [out_ref[s * panel : (s + 1) * panel, :]]
        for number in numbers.values():
            block_rows = jnp.zeros((BLK, width), jnp.float32)
            for block in inner:
                here = out_ref[block * BLK : (block + 1) * BLK, :]
                block_rows = jnp.where(number == block, here, block_rows)
            taken.append(block_rows)
        taken.append(out_ref[(block_count - 1) * BLK :, :])
        gathered = jnp.concatenate(taken, axis=0)
        projected = product3((yth[s], ytl[s]), split(gathered), NN)
        update = product3((lth[s], ltl[s]), split(projected), NN)
        change = product3((yh[s], yl[s]), split(update), NN)
        pieces = [change[k * BLK : (k + 1) * BLK] for k in range(listed_count)]
        fixed = [(s * panel_blocks + k, pieces[k]) for k in range(panel_blocks)]
        for block, piece in fixed + [(block_count - 1, pieces[-1])]:
            out_ref[block * BLK : (block + 1) * BLK, :] -= piece
        for block in inner:
            amount = jnp.zeros((BLK, width), jnp.float32)
            for k, number in numbers.items():
                amount = jnp.where(number == block, pieces[k], amount)
            out_ref[block * BLK : (block + 1) * BLK, :] -= amount
    for s in range(STEPS):
        turned = out_ref[s * panel : (s + 1) * panel, :].T
        projected = product3(split(turned), (uh[s], ul[s]), NN)
        flag = jnp.full(turned.shape, odd[s], jnp.int32)
        tops_ref[pl.ds(first, width), s * panel : (s + 1) * panel] = jnp.where(
            flag == 1, projected, turned
        )


def exchange_kernel(count, listed, odd, m_ref, y_ref, l_ref, u_ref, p_ref, work_ref, g_ref, r_ref, *rest):
    parts = rest[:8]
    t_ref, ring_send, ring_recv, side_send, side_recv, pass_send, pass_recv, a2a_send, a2a_recv, own_sem = rest[8:]
    turn = pl.program_id(0)
    turns = t_ref.shape[0] // m_ref.shape[1]
    me = lax.axis_index("row")
    chips = count // 2
    share = t_ref.shape[0] // count
    core = me % 2
    depth = chips // 2
    lane = (me // 2) % 2
    level = me // 4

    def device(at, on):
        return ((at + depth) % depth * 2 + on) * 2 + core

    partner = me + 1 - 2 * core
    right, left, across = device(level + 1, lane), device(level - 1, lane), device(level, 1 - lane)

    def remote(source, target, send_sem, recv_sem, peer):
        return pltpu.make_async_remote_copy(
            src_ref=source,
            dst_ref=target,
            send_sem=send_sem,
            recv_sem=recv_sem,
            device_id={"row": peer},
            device_id_type=pl.DeviceIdType.MESH,
        )

    ways = [(s, way) for s in range(STEPS) for way in range(2)]
    slots = 2 * depth - 1

    def arrives(way, t):
        return level >= t + 1 if way == 0 else level + t + 1 <= depth - 1

    def leaves(way, t):
        return (level >= t) & (level < depth - 1) if way == 0 else (level + t < depth) & (level > 0)

    def origin_of(way, t):
        return level - t if way == 0 else level + t

    def slot_of(way, t):
        return 1 + t if way == 0 else depth + t

    def hop(s, way, t):
        target = g_ref.at[device(origin_of(way, t), lane), s]
        return remote(
            p_ref.at[s] if t == 0 else target,
            target,
            ring_send.at[s, way, t],
            ring_recv.at[s, way, t],
            right if way == 0 else left,
        )

    def side(s, way, t):
        if t < 0:
            target, slot = g_ref.at[me, s], 0
        else:
            target, slot = g_ref.at[device(origin_of(way, t + 1), lane), s], slot_of(way, t)
        source = p_ref.at[s] if t < 0 else target
        return remote(source, target, side_send.at[s, slot], side_recv.at[s, slot], across)

    def hand(s, way, t, turned):
        on = 1 - lane if turned else lane
        slot = 0 if t < 0 else slot_of(way, t)
        target = g_ref.at[device(level if t < 0 else origin_of(way, t + 1), on), s]
        source = p_ref.at[s] if t < 0 and not turned else target
        slot += slots if turned else 0
        return remote(source, target, pass_send.at[s, slot], pass_recv.at[s, slot], partner)

    def columns_of(peer):
        return t_ref.at[pl.ds(pl.multiple_of(peer * share, 8), share), :]

    def scatter(j):
        peer = (me + j) % count
        return remote(columns_of(peer), r_ref.at[me], a2a_send.at[j - 1], a2a_recv.at[j - 1], peer)

    def keep(s):
        return pltpu.make_async_copy(p_ref.at[s], g_ref.at[me, s], own_sem.at[s])

    def keep_columns():
        return pltpu.make_async_copy(columns_of(me), r_ref.at[me], own_sem.at[STEPS])

    def advance(t):
        for s, way in ways:

            @pl.when(arrives(way, t))
            def _():
                hop(s, way, t).wait_recv()
                if t + 1 < depth - 1:

                    @pl.when(leaves(way, t + 1))
                    def _():
                        hop(s, way, t + 1).start()

                side(s, way, t).start()
                hand(s, way, t, False).start()

    def relay(t):
        for s, way in ways if t >= 0 else [(s, 0) for s in range(STEPS)]:

            def move():
                side(s, way, t).wait_recv()
                hand(s, way, t, True).start()

            if t < 0:
                move()
            else:
                pl.when(arrives(way, t))(move)

    def finish(t):
        for s, way in ways if t >= 0 else [(s, 0) for s in range(STEPS)]:

            def end():
                side(s, way, t).wait_send()
                hand(s, way, t, False).wait()
                hand(s, way, t, True).wait()

            if t < 0:
                end()
            else:
                pl.when(arrives(way, t))(end)

                @pl.when(leaves(way, t))
                def _():
                    hop(s, way, t).wait_send()

    @pl.when(turn == 0)
    def _():
        barrier = pltpu.get_barrier_semaphore()
        for j in range(1, count):
            pl.semaphore_signal(
                barrier,
                inc=1,
                device_id={"row": (me + j) % count},
                device_id_type=pl.DeviceIdType.MESH,
            )
        pl.semaphore_wait(barrier, count - 1)
        for s, way in ways:

            @pl.when(leaves(way, 0))
            def _():
                hop(s, way, 0).start()

        for s in range(STEPS):
            side(s, 0, -1).start()
            hand(s, 0, -1, False).start()
            keep(s).start()
        yh, yl, yth, ytl, lth, ltl, uh, ul = parts
        for s in range(STEPS):
            yh[s], yl[s] = split(y_ref[s])
            yth[s], ytl[s] = split(y_ref[s].T)
            lth[s], ltl[s] = split(l_ref[s].T)
            uh[s], ul[s] = split(u_ref[s])

    first = pl.multiple_of(turn * m_ref.shape[1], m_ref.shape[1])
    leaf_block(listed, odd, m_ref, u_ref, work_ref, t_ref, first, parts)

    early = min(turns - 1, depth - 1)
    for t in range(early):

        @pl.when(turn == t)
        def _():
            advance(t)
            relay(t - 1)

    @pl.when(turn == turns - 1)
    def _():
        for t in range(early, depth - 1):
            advance(t)
            relay(t - 1)
        todo = [(j + count // 2 - 1) % (count - 1) + 1 for j in range(count - 1)]
        keep_columns().start()
        for j in todo:
            scatter(j).start()
        relay(depth - 2)
        for t in range(-1, depth - 1):
            finish(t)
        for s in range(STEPS):
            keep(s).wait()
        keep_columns().wait()
        for j in todo:
            scatter(j).wait()


def exchange(count, matrix, leaf_vectors, leaf_factors, tree_vectors, packed, leaf_blocks, odd):
    rows, columns = matrix.shape
    width = COLS_PER_LEAF
    steps, leaf_rows, panel = leaf_vectors.shape
    chips = count // 2
    dma = pltpu.SemaphoreType.DMA
    half_type = jnp.bfloat16

    def whole(array):
        return pl.BlockSpec(array.shape, lambda c, *_: (0, 0, 0))

    return pl.pallas_call(
        functools.partial(exchange_kernel, count),
        out_shape=(
            jax.ShapeDtypeStruct((rows, columns), jnp.float32),
            jax.ShapeDtypeStruct((count,) + packed.shape, jnp.float32),
            jax.ShapeDtypeStruct((count, columns // count, steps * panel), jnp.float32),
        ),
        grid_spec=pltpu.PrefetchScalarGridSpec(
            num_scalar_prefetch=2,
            grid=(columns // width,),
            in_specs=[
                pl.BlockSpec((rows, width), lambda c, *_: (0, c)),
                whole(leaf_vectors),
                whole(leaf_factors),
                whole(tree_vectors),
                whole(packed),
            ],
            out_specs=[
                pl.BlockSpec((rows, width), lambda c, *_: (0, c)),
                pl.BlockSpec(memory_space=pl.ANY),
                pl.BlockSpec(memory_space=pl.ANY),
            ],
            scratch_shapes=[
                *[pltpu.VMEM((steps, leaf_rows, panel), half_type)] * 2,
                *[pltpu.VMEM((steps, panel, leaf_rows), half_type)] * 2,
                *[pltpu.VMEM((steps, panel, panel), half_type)] * 4,
                pltpu.VMEM((columns, steps * panel), jnp.float32),
                dma((steps, 2, chips // 2)),
                dma((steps, 2, chips // 2)),
                dma((steps, chips - 1)),
                dma((steps, chips - 1)),
                dma((steps, 2 * chips - 2)),
                dma((steps, 2 * chips - 2)),
                dma((count - 1,)),
                dma((count - 1,)),
                dma((steps + 1,)),
            ],
        ),
        compiler_params=pltpu.CompilerParams(collective_id=0, has_side_effects=True),
    )(leaf_blocks, odd, matrix, leaf_vectors, leaf_factors, tree_vectors, packed)


def tree_kernel(upper, lower, x_ref, g_ref, out_ref):
    node = pl.program_id(0)
    panel = g_ref.shape[2]
    half = panel // 2
    first_level = x_ref.shape[0] // 2

    @pl.when(node == 0)
    def _():
        out_ref[...] = x_ref[...]

    a, b = upper[node], lower[node]
    slot = lax.rem(b, 2)
    above, on = corner_masks(half)
    corner = g_ref[slot, half : 2 * half, :half]
    diagonal = g_ref[slot, 2 * half : 2 * half + 1, :half]
    top = jnp.concatenate(
        [jnp.where(above | on, corner, 0.0), g_ref[slot, half : 2 * half, half:]], axis=1
    )
    last = jnp.where(above, corner.T, jnp.where(on, diagonal, 0.0))
    bottom = jnp.concatenate([jnp.zeros_like(last), last], axis=1)
    f = split(jnp.concatenate([top, bottom], axis=0))
    xa, xb = out_ref[a], out_ref[b]

    @pl.when(node < first_level)
    def _():
        w = product3(split(xa + xb), f, NN)
        out_ref[a] = xa - w
        out_ref[b] = w

    @pl.when(node >= first_level)
    def _():
        u = split(jnp.concatenate([g_ref[0, :half, :], g_ref[1, :half, :]], axis=0))
        w = product3(split(xa + product3(split(xb), u, NN)), f, NN)
        out_ref[a] = xa - w
        out_ref[b] = xb - product3(split(w), u, NT)


def tree(step, spread, reflectors, upper, lower):
    devices, width, both = spread.shape
    block = (devices, width, both // STEPS)
    return pl.pallas_call(
        tree_kernel,
        out_shape=jax.ShapeDtypeStruct(block, jnp.float32),
        grid_spec=pltpu.PrefetchScalarGridSpec(
            num_scalar_prefetch=2,
            grid=(devices - 1,),
            in_specs=[
                pl.BlockSpec(block, lambda n, *_: (0, 0, step)),
                pl.BlockSpec(
                    (2, None) + reflectors.shape[2:], lambda n, up, lo: (lo[n] // 2, step, 0, 0)
                ),
            ],
            out_specs=pl.BlockSpec(block, lambda n, *_: (0, 0, 0)),
        ),
    )(upper, lower, spread, reflectors)


def place_rows(flag, back_ref, u_ref, rows_ref, out_ref):
    @pl.when(flag == 0)
    def _():
        out_ref[...] = back_ref[...].T

    @pl.when(flag == 1)
    def _():
        out_ref[...] = rows_ref[...] - product3(split(u_ref[...]), split(back_ref[...]), NT)


def place_kernel(odd, back_ref, u_ref, work_ref, out_ref):
    panel = u_ref.shape[0]
    rows = out_ref.shape[0]
    place_rows(odd[0], back_ref, u_ref, work_ref.at[:panel], out_ref.at[:panel])
    if rows > panel:
        out_ref[panel:, :] = work_ref[panel:, :]


def place(step, back, vectors, work, odd):
    columns, panel = back.shape
    width = COLS_PER_LEAF
    rows = work.shape[0] if step == 0 else panel
    return pl.pallas_call(
        place_kernel,
        out_shape=jax.ShapeDtypeStruct(work.shape, jnp.float32),
        grid_spec=pltpu.PrefetchScalarGridSpec(
            num_scalar_prefetch=1,
            grid=(columns // width,),
            in_specs=[
                pl.BlockSpec((width, panel), lambda c, *_: (c, 0)),
                pl.BlockSpec((panel, panel), lambda c, *_: (0, 0)),
                pl.BlockSpec((rows, width), lambda c, *_: (step, c)),
            ],
            out_specs=pl.BlockSpec((rows, width), lambda c, *_: (step, c)),
        ),
        input_output_aliases={} if step == 0 else {3: 0},
    )(odd, back, vectors, work)


def pairs(row_count):
    uppers, lowers = [], []
    gap = 1
    while gap < row_count:
        for start in range(0, row_count, 2 * gap):
            uppers.append(start)
            lowers.append(start + gap)
        gap *= 2
    return jnp.array(uppers, jnp.int32), jnp.array(lowers, jnp.int32)


def shards(matrix, leaf_vectors, leaf_factors, tree_vectors, tree_factors, leaf_blocks, owner):
    row_count = lax.axis_size("row")
    my_index = lax.axis_index("row")
    columns = matrix.shape[1]
    panel = tree_vectors.shape[2]
    half = panel // 2
    core = my_index % 2
    odd = ((my_index - owner) % 2).astype(jnp.int32)
    own = lax.dynamic_slice_in_dim(tree_vectors, core * half, half, axis=1)
    asked = lax.dynamic_slice_in_dim(tree_vectors, (1 - core) * half, half, axis=1)
    other = lax.ppermute(asked, "row", [(i, i ^ 1) for i in range(row_count)])
    packed = pack(own, other, tree_factors, odd)
    work, reflectors, spread = exchange(
        row_count, matrix, leaf_vectors, leaf_factors, tree_vectors, packed, leaf_blocks, odd
    )
    uppers, lowers = pairs(row_count)
    for s in range(STEPS):
        upper, lower = (uppers + owner[s]) % row_count, (lowers + owner[s]) % row_count
        done = tree(s, spread, reflectors, upper, lower)
        back = lax.all_to_all(done, "row", 0, 0).reshape(columns, panel)
        work = place(s, back, tree_vectors[s], work, odd[s : s + 1])
    return work


def solution(mesh):
    return jax.shard_map(
        shards,
        mesh=mesh,
        in_specs=(
            P(("groups", "row"), None),
            P("groups", "row", None),
            P("groups", "row", None),
            P("groups", "row", None),
            P("groups", "row", None),
            P("groups", "row"),
            P("groups"),
        ),
        out_specs=P(("groups", "row"), None),
        check_vma=False,
    )
```

```python
import functools

import jax
import jax.numpy as jnp
from jax import lax
from jax.experimental import pallas as pl
from jax.experimental.pallas import tpu as pltpu
from jax.sharding import PartitionSpec as P

BLK = 128
STEPS = 2
COLS_PER_LEAF = 256

NN = (((1,), (0,)), ((), ()))
TN = (((0,), (0,)), ((), ()))
NT = (((1,), (1,)), ((), ()))


def split(value):
    high = value.astype(jnp.bfloat16)
    low = (value - high.astype(jnp.float32)).astype(jnp.bfloat16)
    return high, low


def product3(left, right, dims):
    def one(a, b):
        return lax.dot_general(a, b, dims, preferred_element_type=jnp.float32)

    return one(left[0], right[0]) + (one(left[0], right[1]) + one(left[1], right[0]))


def corner_masks(half):
    row = lax.broadcasted_iota(jnp.int32, (half, half), 0)
    column = lax.broadcasted_iota(jnp.int32, (half, half), 1)
    return row < column, row == column


def pack_kernel(odd, own_ref, other_ref, f_ref, all_ref):
    half = own_ref.shape[1]
    above, on = corner_masks(half)
    for s in range(STEPS):
        out_ref = all_ref.at[s]
        out_ref[:half, :] = own_ref[s]

        @pl.when(odd[s] == 1)
        def _():
            out_ref[:half, :] = other_ref[s]

        first = f_ref[s, :half, :half]
        second = f_ref[s, half:, half:]
        out_ref[half : 2 * half, :half] = jnp.where(above | on, first, second.T)
        out_ref[half : 2 * half, half:] = f_ref[s, :half, half:]
        diagonal = jnp.sum(jnp.where(on, second, 0.0), axis=0, keepdims=True)
        line = jnp.concatenate([diagonal, jnp.zeros_like(diagonal)], axis=1)
        out_ref[2 * half :, :] = jnp.broadcast_to(line, (8, 2 * half))


def pack(own, other, factors, odd):
    steps, half, panel = own.shape
    shape = (steps, panel + 8, panel)
    return pl.pallas_call(
        pack_kernel,
        out_shape=jax.ShapeDtypeStruct(shape, jnp.float32),
        grid_spec=pltpu.PrefetchScalarGridSpec(
            num_scalar_prefetch=1,
            grid=(1,),
            in_specs=[
                pl.BlockSpec(own.shape, lambda c, *_: (0, 0, 0)),
                pl.BlockSpec(other.shape, lambda c, *_: (0, 0, 0)),
                pl.BlockSpec(factors.shape, lambda c, *_: (0, 0, 0)),
            ],
            out_specs=pl.BlockSpec(shape, lambda c, *_: (0, 0, 0)),
        ),
    )(odd, own, other, factors)


def chip_at(place, chips):
    return jnp.where(place < chips // 2, 2 * place, 2 * (chips - 1 - place) + 1)


def place_of(chip, chips):
    return jnp.where(chip % 2 == 0, chip // 2, chips - 1 - chip // 2)


def leaf_block(listed, odd, m_ref, u_ref, out_ref, tops_ref, first, parts):
    yh, yl, yth, ytl, lth, ltl, uh, ul = parts
    panel = u_ref.shape[1]
    width = out_ref.shape[1]
    block_count = out_ref.shape[0] // BLK
    listed_count = yh.shape[1] // BLK
    panel_blocks = panel // BLK
    out_ref[...] = m_ref[...]
    for s in range(STEPS):
        inner = range((s + 1) * panel_blocks, block_count - 1)
        numbers = {
            k: jnp.full((BLK, width), listed[s, k], jnp.int32)
            for k in range(panel_blocks, listed_count - 1)
        }
        taken = [out_ref[s * panel : (s + 1) * panel, :]]
        for number in numbers.values():
            block_rows = jnp.zeros((BLK, width), jnp.float32)
            for block in inner:
                here = out_ref[block * BLK : (block + 1) * BLK, :]
                block_rows = jnp.where(number == block, here, block_rows)
            taken.append(block_rows)
        taken.append(out_ref[(block_count - 1) * BLK :, :])
        gathered = jnp.concatenate(taken, axis=0)
        projected = product3((yth[s], ytl[s]), split(gathered), NN)
        update = product3((lth[s], ltl[s]), split(projected), NN)
        change = product3((yh[s], yl[s]), split(update), NN)
        pieces = [change[k * BLK : (k + 1) * BLK] for k in range(listed_count)]
        fixed = [(s * panel_blocks + k, pieces[k]) for k in range(panel_blocks)]
        for block, piece in fixed + [(block_count - 1, pieces[-1])]:
            out_ref[block * BLK : (block + 1) * BLK, :] -= piece
        for block in inner:
            amount = jnp.zeros((BLK, width), jnp.float32)
            for k, number in numbers.items():
                amount = jnp.where(number == block, pieces[k], amount)
            out_ref[block * BLK : (block + 1) * BLK, :] -= amount
    for s in range(STEPS):
        turned = out_ref[s * panel : (s + 1) * panel, :].T
        projected = product3(split(turned), (uh[s], ul[s]), NN)
        flag = jnp.full(turned.shape, odd[s], jnp.int32)
        tops_ref[pl.ds(first, width), s * panel : (s + 1) * panel] = jnp.where(
            flag == 1, projected, turned
        )


def exchange_kernel(count, listed, odd, m_ref, y_ref, l_ref, u_ref, p_ref, work_ref, g_ref, r_ref, *rest):
    parts = rest[:8]
    t_ref, ring_send, ring_recv, pass_send, pass_recv, a2a_send, a2a_recv, own_sem = rest[8:]
    turn = pl.program_id(0)
    turns = t_ref.shape[0] // m_ref.shape[1]
    me = lax.axis_index("row")
    chips = count // 2
    share = t_ref.shape[0] // count
    core = me % 2
    place = place_of(me // 2, chips)

    def device(offset):
        return chip_at((place + offset + chips) % chips, chips) * 2 + core

    partner = me + 1 - 2 * core
    right, left = device(1), device(-1)

    def remote(source, target, send_sem, recv_sem, peer):
        return pltpu.make_async_remote_copy(
            src_ref=source,
            dst_ref=target,
            send_sem=send_sem,
            recv_sem=recv_sem,
            device_id={"row": peer},
            device_id_type=pl.DeviceIdType.MESH,
        )

    lengths = {(0, 0): chips // 2, (0, 1): chips - 1 - chips // 2}
    lengths[1, 1], lengths[1, 0] = lengths[0, 0], lengths[0, 1]
    longest = max(lengths.values())

    def hop(s, way, t):
        origin = device(-t if way == 0 else t)
        source = p_ref.at[s] if t == 0 else g_ref.at[origin, s]
        return remote(
            source,
            g_ref.at[origin, s],
            ring_send.at[s, way, t],
            ring_recv.at[s, way, t],
            right if way == 0 else left,
        )

    def hand(s, way, t):
        if t < 0:
            return remote(
                p_ref.at[s], g_ref.at[me, s], pass_send.at[s, 0], pass_recv.at[s, 0], partner
            )
        origin = device(-t - 1 if way == 0 else t + 1)
        slot = 1 + (t if way == 0 else lengths[s, 0] + t)
        piece = g_ref.at[origin, s]
        return remote(piece, piece, pass_send.at[s, slot], pass_recv.at[s, slot], partner)

    def columns_of(peer):
        return t_ref.at[pl.ds(pl.multiple_of(peer * share, 8), share), :]

    def scatter(j):
        peer = (me + j) % count
        return remote(columns_of(peer), r_ref.at[me], a2a_send.at[j - 1], a2a_recv.at[j - 1], peer)

    def keep(s):
        return pltpu.make_async_copy(p_ref.at[s], g_ref.at[me, s], own_sem.at[s])

    def keep_columns():
        return pltpu.make_async_copy(columns_of(me), r_ref.at[me], own_sem.at[STEPS])

    def advance(t):
        for s, way in lengths:
            if t < lengths[s, way]:
                hop(s, way, t).wait_recv()
                if t + 1 < lengths[s, way]:
                    hop(s, way, t + 1).start()
                hand(s, way, t).start()

    @pl.when(turn == 0)
    def _():
        barrier = pltpu.get_barrier_semaphore()
        for j in range(1, count):
            pl.semaphore_signal(
                barrier,
                inc=1,
                device_id={"row": (me + j) % count},
                device_id_type=pl.DeviceIdType.MESH,
            )
        pl.semaphore_wait(barrier, count - 1)
        for s, way in lengths:
            if lengths[s, way] > 0:
                hop(s, way, 0).start()
        for s in range(STEPS):
            hand(s, 0, -1).start()
            keep(s).start()
        yh, yl, yth, ytl, lth, ltl, uh, ul = parts
        for s in range(STEPS):
            yh[s], yl[s] = split(y_ref[s])
            yth[s], ytl[s] = split(y_ref[s].T)
            lth[s], ltl[s] = split(l_ref[s].T)
            uh[s], ul[s] = split(u_ref[s])

    first = pl.multiple_of(turn * m_ref.shape[1], m_ref.shape[1])
    leaf_block(listed, odd, m_ref, u_ref, work_ref, t_ref, first, parts)

    early = min(turns - 1, longest)
    for t in range(early):

        @pl.when(turn == t)
        def _():
            advance(t)

    @pl.when(turn == turns - 1)
    def _():
        todo = [(j + count // 2 - 1) % (count - 1) + 1 for j in range(count - 1)]
        rounds = max(longest - early, 1)
        size = -(-len(todo) // rounds)
        keep_columns().start()
        for t in range(rounds):
            for j in todo[t * size : (t + 1) * size]:
                scatter(j).start()
            advance(early + t)
        for s, way in lengths:
            for t in range(lengths[s, way]):
                hop(s, way, t).wait_send()
                hand(s, way, t).wait()
        for s in range(STEPS):
            hand(s, 0, -1).wait()
            keep(s).wait()
        keep_columns().wait()
        for j in todo:
            scatter(j).wait()


def exchange(count, matrix, leaf_vectors, leaf_factors, tree_vectors, packed, leaf_blocks, odd):
    rows, columns = matrix.shape
    width = COLS_PER_LEAF
    steps, leaf_rows, panel = leaf_vectors.shape
    chips = count // 2
    dma = pltpu.SemaphoreType.DMA
    half_type = jnp.bfloat16

    def whole(array):
        return pl.BlockSpec(array.shape, lambda c, *_: (0, 0, 0))

    return pl.pallas_call(
        functools.partial(exchange_kernel, count),
        out_shape=(
            jax.ShapeDtypeStruct((rows, columns), jnp.float32),
            jax.ShapeDtypeStruct((count,) + packed.shape, jnp.float32),
            jax.ShapeDtypeStruct((count, columns // count, steps * panel), jnp.float32),
        ),
        grid_spec=pltpu.PrefetchScalarGridSpec(
            num_scalar_prefetch=2,
            grid=(columns // width,),
            in_specs=[
                pl.BlockSpec((rows, width), lambda c, *_: (0, c)),
                whole(leaf_vectors),
                whole(leaf_factors),
                whole(tree_vectors),
                whole(packed),
            ],
            out_specs=[
                pl.BlockSpec((rows, width), lambda c, *_: (0, c)),
                pl.BlockSpec(memory_space=pl.ANY),
                pl.BlockSpec(memory_space=pl.ANY),
            ],
            scratch_shapes=[
                *[pltpu.VMEM((steps, leaf_rows, panel), half_type)] * 2,
                *[pltpu.VMEM((steps, panel, leaf_rows), half_type)] * 2,
                *[pltpu.VMEM((steps, panel, panel), half_type)] * 4,
                pltpu.VMEM((columns, steps * panel), jnp.float32),
                dma((steps, 2, chips)),
                dma((steps, 2, chips)),
                dma((steps, chips)),
                dma((steps, chips)),
                dma((count - 1,)),
                dma((count - 1,)),
                dma((steps + 1,)),
            ],
        ),
        compiler_params=pltpu.CompilerParams(collective_id=0, has_side_effects=True),
    )(leaf_blocks, odd, matrix, leaf_vectors, leaf_factors, tree_vectors, packed)


def tree_kernel(upper, lower, x_ref, g_ref, out_ref):
    node = pl.program_id(0)
    panel = g_ref.shape[2]
    half = panel // 2
    first_level = x_ref.shape[0] // 2

    @pl.when(node == 0)
    def _():
        out_ref[...] = x_ref[...]

    a, b = upper[node], lower[node]
    slot = lax.rem(b, 2)
    above, on = corner_masks(half)
    corner = g_ref[slot, half : 2 * half, :half]
    diagonal = g_ref[slot, 2 * half : 2 * half + 1, :half]
    top = jnp.concatenate(
        [jnp.where(above | on, corner, 0.0), g_ref[slot, half : 2 * half, half:]], axis=1
    )
    last = jnp.where(above, corner.T, jnp.where(on, diagonal, 0.0))
    bottom = jnp.concatenate([jnp.zeros_like(last), last], axis=1)
    f = split(jnp.concatenate([top, bottom], axis=0))
    xa, xb = out_ref[a], out_ref[b]

    @pl.when(node < first_level)
    def _():
        w = product3(split(xa + xb), f, NN)
        out_ref[a] = xa - w
        out_ref[b] = w

    @pl.when(node >= first_level)
    def _():
        u = split(jnp.concatenate([g_ref[0, :half, :], g_ref[1, :half, :]], axis=0))
        w = product3(split(xa + product3(split(xb), u, NN)), f, NN)
        out_ref[a] = xa - w
        out_ref[b] = xb - product3(split(w), u, NT)


def tree(step, spread, reflectors, upper, lower):
    devices, width, both = spread.shape
    block = (devices, width, both // STEPS)
    return pl.pallas_call(
        tree_kernel,
        out_shape=jax.ShapeDtypeStruct(block, jnp.float32),
        grid_spec=pltpu.PrefetchScalarGridSpec(
            num_scalar_prefetch=2,
            grid=(devices - 1,),
            in_specs=[
                pl.BlockSpec(block, lambda n, *_: (0, 0, step)),
                pl.BlockSpec(
                    (2, None) + reflectors.shape[2:], lambda n, up, lo: (lo[n] // 2, step, 0, 0)
                ),
            ],
            out_specs=pl.BlockSpec(block, lambda n, *_: (0, 0, 0)),
        ),
    )(upper, lower, spread, reflectors)


def place_rows(flag, back_ref, u_ref, rows_ref, out_ref):
    @pl.when(flag == 0)
    def _():
        out_ref[...] = back_ref[...].T

    @pl.when(flag == 1)
    def _():
        out_ref[...] = rows_ref[...] - product3(split(u_ref[...]), split(back_ref[...]), NT)


def place_kernel(odd, back_ref, u_ref, work_ref, out_ref):
    panel = u_ref.shape[0]
    rows = out_ref.shape[0]
    place_rows(odd[0], back_ref, u_ref, work_ref.at[:panel], out_ref.at[:panel])
    if rows > panel:
        out_ref[panel:, :] = work_ref[panel:, :]


def place(step, back, vectors, work, odd):
    columns, panel = back.shape
    width = COLS_PER_LEAF
    rows = work.shape[0] if step == 0 else panel
    return pl.pallas_call(
        place_kernel,
        out_shape=jax.ShapeDtypeStruct(work.shape, jnp.float32),
        grid_spec=pltpu.PrefetchScalarGridSpec(
            num_scalar_prefetch=1,
            grid=(columns // width,),
            in_specs=[
                pl.BlockSpec((width, panel), lambda c, *_: (c, 0)),
                pl.BlockSpec((panel, panel), lambda c, *_: (0, 0)),
                pl.BlockSpec((rows, width), lambda c, *_: (step, c)),
            ],
            out_specs=pl.BlockSpec((rows, width), lambda c, *_: (step, c)),
        ),
        input_output_aliases={} if step == 0 else {3: 0},
    )(odd, back, vectors, work)


def pairs(row_count):
    uppers, lowers = [], []
    gap = 1
    while gap < row_count:
        for start in range(0, row_count, 2 * gap):
            uppers.append(start)
            lowers.append(start + gap)
        gap *= 2
    return jnp.array(uppers, jnp.int32), jnp.array(lowers, jnp.int32)


def shards(matrix, leaf_vectors, leaf_factors, tree_vectors, tree_factors, leaf_blocks, owner):
    row_count = lax.axis_size("row")
    my_index = lax.axis_index("row")
    columns = matrix.shape[1]
    panel = tree_vectors.shape[2]
    half = panel // 2
    core = my_index % 2
    odd = ((my_index - owner) % 2).astype(jnp.int32)
    own = lax.dynamic_slice_in_dim(tree_vectors, core * half, half, axis=1)
    asked = lax.dynamic_slice_in_dim(tree_vectors, (1 - core) * half, half, axis=1)
    other = lax.ppermute(asked, "row", [(i, i ^ 1) for i in range(row_count)])
    packed = pack(own, other, tree_factors, odd)
    work, reflectors, spread = exchange(
        row_count, matrix, leaf_vectors, leaf_factors, tree_vectors, packed, leaf_blocks, odd
    )
    uppers, lowers = pairs(row_count)
    for s in range(STEPS):
        upper, lower = (uppers + owner[s]) % row_count, (lowers + owner[s]) % row_count
        done = tree(s, spread, reflectors, upper, lower)
        back = lax.all_to_all(done, "row", 0, 0).reshape(columns, panel)
        work = place(s, back, tree_vectors[s], work, odd[s : s + 1])
    return work


def solution(mesh):
    return jax.shard_map(
        shards,
        mesh=mesh,
        in_specs=(
            P(("groups", "row"), None),
            P("groups", "row", None),
            P("groups", "row", None),
            P("groups", "row", None),
            P("groups", "row", None),
            P("groups", "row"),
            P("groups"),
        ),
        out_specs=P(("groups", "row"), None),
        check_vma=False,
    )
```
